32 devices in a mesh: space: 4 (over z), vel: 8 (over y, x, core).
Axes of the slice: x: 2, y: 2, z: 4, core: 2. Of those that a mesh axis runs over, the one named last changes fastest.
Arguments:
- dist: float32 [64, 16, 16, 2048], P('space', None, None, 'vel'), may hold values from 0.05 to 2
- relax_rate: float32 [64, 16, 16], P('space'), may hold values from 0.2 to 0.9
- kinetic_cells: int32 [2, 16384], P(None, 'space'), may hold values from 0 to 4095, as said below
- kinetic_count: int32 [2, 4], replicated, may hold values from 1 to 4096, 8192 in all within a row
- map_a: bfloat16 [2048, 768], replicated, may hold values from -0.125 to 0.125
- map_b: bfloat16 [2048, 768], replicated, may hold values from -0.125 to 0.125
- map_c: bfloat16 [768, 2048], replicated, may hold values from -0.21875 to 0.21875
Outputs:
- dist_out: float32 [64, 16, 16, 2048], P('space', None, None, 'vel')
The draws below stay inside these ranges and needn't reach their ends.
Inputs may be any that keep to these rules, and one draw needn't show every extreme that they name: `kinetic_cells`: for each step, the 4096 entries of a slab's block are a permutation of that slab's local cell numbers. `kinetic_count`: each step's counts sum to 8192, and one slab is kinetic in all its cells.
All inputs are finite; a program needn't handle non-finite values.
Results may differ from the reference program's by a relative error of at most 0.0034.
Values may be sent and summed in bfloat16 or wider, within the bound.
A program may use at most 128 MiB of HBM per device.

```python
import math
import jax
import jax.numpy as jnp
import numpy as np
from jax import lax

GX = 16
GY = 16
GZ = 8
RANK = 768
STEPS = 2
CX = 16
NY = 16
NZ = 16
NV = 2048
NX = 64
KMEAN = 2048
KTOT = 8192
N_SPACE = 4
N_VEL = 8


def draw_kinetic_cells(key, part):
    block_keys = jax.random.split(jax.random.fold_in(key, 17), STEPS * N_SPACE)
    chosen = jax.vmap(lambda one_key: jax.random.permutation(one_key, CX * NY * NZ))(block_keys)
    return chosen.reshape(STEPS, N_SPACE * CX * NY * NZ).astype(jnp.int32)


def levels(key, dims, cuts, least, top_value):
    def one(dim, blocks):
        heights = jax.random.uniform(jax.random.fold_in(jax.random.fold_in(key, 6), dim), (blocks,), jnp.float32, least / len(cuts), top_value / len(cuts))
        return jnp.repeat(jnp.exp(heights), dims[dim] // blocks).reshape((-1,) + (1,) * (len(dims) - dim - 1))

    factor_of = one(*cuts[0])
    for cut in cuts[1:]:
        factor_of = factor_of * one(*cut)
    return factor_of


def profile(number_of, total, most, lean):
    loads = [(1 << 20) // math.isqrt(grade ** lean) + 1 for grade in range(2, number_of + 1)]
    spare, given = total - most - (number_of - 1), [1] * (number_of - 1)
    while spare > 0:
        free = [i for i in range(number_of - 1) if given[i] < most]
        pool, left = sum([loads[i] for i in free]), spare
        for i in free:
            more = min(most - given[i], max(1, left * loads[i] // pool), spare)
            given[i] = given[i] + more
            spare = spare - more
    return np.array([most] + given)


def uneven(rng, number_of, total, bound, slope):
    if number_of == 2:
        one = jax.random.randint(rng, (), max(1, total - bound), min(bound, total - 1) + 1)
        return jnp.stack([one, total - one])
    sizes = jnp.asarray(profile(number_of, total, bound, slope), jnp.int32)
    pairs = (number_of - 1) // 2
    donor, sink = sizes[1:1 + 2 * pairs:2], sizes[2:2 + 2 * pairs:2]
    slack = jnp.minimum(donor - 1, bound - sink)
    moved = jax.random.randint(jax.random.fold_in(rng, 1), (pairs,), 0, 1 << 20) % (slack + 1)
    sizes = sizes.at[1:1 + 2 * pairs:2].set(donor - moved).at[2:2 + 2 * pairs:2].set(sink + moved)
    return sizes[jax.random.permutation(jax.random.fold_in(rng, 2), number_of)]


def centred(key, dims, scale, limit, held_as=jnp.bfloat16):
    result = jax.random.normal(key, dims, jnp.float32) * scale
    return jnp.minimum(jnp.maximum(result, -limit), limit).astype(held_as)


def setup_inputs(seed: int = 0) -> dict:
    key_list = jax.random.split(jax.random.key(seed), 8)
    dist = jnp.clip(jnp.exp(math.log(2.0) - 3.6888794 * jax.random.uniform(key_list[0], (NX, NY, NZ, NV), jnp.float32) ** levels(key_list[0], (NX, NY, NZ, NV), ((0, 4), (3, 8)), -0.2, 0.2)), 0.05, 2.0)
    relax_rate = jnp.clip(0.2 + 0.7 * jax.random.uniform(key_list[1], (NX, NY, NZ), jnp.float32) ** levels(key_list[1], (NX, NY, NZ), ((0, 4),), -0.2, 0.2), 0.2, 0.9)
    kinetic_cells = draw_kinetic_cells(jax.random.fold_in(key_list[7], 71), 0)
    kinetic_count = jax.vmap(lambda own: uneven(own, N_SPACE, KTOT, CX * NY * NZ, 2))(jax.random.split(key_list[3], STEPS)).reshape((STEPS, N_SPACE)).astype(jnp.int32)
    map_a = centred(key_list[4], (NV, RANK), NV ** -0.5, 0.125)
    map_b = centred(key_list[5], (NV, RANK), NV ** -0.5, 0.125)
    map_c = centred(key_list[6], (RANK, NV), RANK ** -0.5, 0.21875)
    return dict(dist=dist, relax_rate=relax_rate, kinetic_cells=kinetic_cells, kinetic_count=kinetic_count, map_a=map_a, map_b=map_b, map_c=map_c)


COURANT = 0.1
SPACING = 0.5
COLLIDE = 0.5


def velocity_tables():
    grid_index = jnp.arange(GX * GY * GZ, dtype=jnp.int32)
    along_x = ((grid_index // (GY * GZ)).astype(jnp.float32) - 0.5 * (GX - 1)) * SPACING
    along_y = (((grid_index // GZ) % GY).astype(jnp.float32) - 0.5 * (GY - 1)) * SPACING
    along_z = ((grid_index % GZ).astype(jnp.float32) - 0.5 * (GZ - 1)) * SPACING
    speed_sq = along_x * along_x + along_y * along_y + along_z * along_z
    weights = jnp.exp(-0.5 * speed_sq)
    weights = weights / jnp.sum(weights)
    moment_basis = jnp.stack([jnp.ones_like(along_x), along_x, along_y, along_z, speed_sq])
    consts = (jnp.sum(weights * along_x * along_x), jnp.sum(weights * along_y * along_y),
              jnp.sum(weights * along_z * along_z), jnp.sum(weights * speed_sq),
              jnp.sum(weights * speed_sq * speed_sq))
    return moment_basis, moment_basis * weights[None, :], consts


def coefficients(moments, consts):
    thermal = (moments[4] - consts[3] * moments[0]) / (consts[4] - consts[3] * consts[3])
    return jnp.stack([moments[0] - consts[3] * thermal, moments[1] / consts[0],
                      moments[2] / consts[1], moments[3] / consts[2], thermal])


def limited_slope(first_diff, second_diff):
    return 0.5 * (jnp.sign(first_diff) + jnp.sign(second_diff)) * jnp.minimum(jnp.abs(first_diff), jnp.abs(second_diff))


def face_flux(padded, velocity, direction):
    extent = padded.shape[direction] - 4
    def window(array, offset, amount):
        return lax.slice_in_dim(array, offset, offset + amount, axis=direction)
    diffs = window(padded, 1, extent + 3) - window(padded, 0, extent + 3)
    left_state = window(padded, 1, extent + 1) + 0.5 * limited_slope(window(diffs, 0, extent + 1), window(diffs, 1, extent + 1))
    right_state = window(padded, 2, extent + 1) - 0.5 * limited_slope(window(diffs, 1, extent + 1), window(diffs, 2, extent + 1))
    fluxes = jnp.maximum(velocity, 0.0) * left_state + jnp.minimum(velocity, 0.0) * right_state
    return window(fluxes, 1, extent) - window(fluxes, 0, extent)


def periodic_pad(current, direction):
    extent = current.shape[direction]
    return jnp.concatenate([lax.slice_in_dim(current, extent - 2, extent, axis=direction), current,
                            lax.slice_in_dim(current, 0, 2, axis=direction)], axis=direction)


def transport(padded, current, speed_x, speed_y, speed_z):
    change = face_flux(padded, speed_x, 0) + face_flux(periodic_pad(current, 1), speed_y, 1)
    change = change + face_flux(periodic_pad(current, 2), speed_z, 2)
    return current - COURANT * change


def collide(row_block, map_a, map_b, map_c):
    first_map = jnp.dot(row_block, map_a, preferred_element_type=jnp.float32)
    second_map = jnp.dot(row_block, map_b, preferred_element_type=jnp.float32)
    hidden = (first_map * second_map).astype(jnp.bfloat16)
    return jnp.dot(hidden, map_c, preferred_element_type=jnp.float32).astype(jnp.bfloat16)


def reference(dist, relax_rate, kinetic_cells, kinetic_count, map_a, map_b, map_c):
    vel_width = NV // N_VEL
    moment_basis, weighted, consts = velocity_tables()
    cell_total = NX * NY * NZ
    slab_cells = cell_total // N_SPACE
    current = jnp.moveaxis(dist.reshape(NX, NY, NZ, N_VEL, vel_width), 3, 0)
    speeds = moment_basis[1:4].reshape(3, N_VEL, vel_width)
    grouped_basis = moment_basis.reshape(5, N_VEL, vel_width)
    grouped_weighted = weighted.reshape(5, N_VEL, vel_width)
    relax_rows = relax_rate.reshape(1, cell_total, 1)
    for step_index in range(STEPS):
        advected = lax.map(lambda member: transport(periodic_pad(member[0], 0), member[0], member[1], member[2], member[3]),
                           (current, speeds[0], speeds[1], speeds[2]))
        flat_rows = advected.reshape(N_VEL, cell_total, vel_width)
        moments = jnp.einsum("mgv,gcv->mc", grouped_basis, flat_rows, precision=lax.Precision.HIGHEST)
        coeffs = coefficients(moments, consts)
        equilibrium = jnp.einsum("mc,mgv->gcv", coeffs, grouped_weighted, precision=lax.Precision.HIGHEST)
        relaxed = flat_rows + relax_rows * (equilibrium - flat_rows)
        slab_counts = kinetic_count[step_index].astype(jnp.int32)
        slab_ends = jnp.cumsum(slab_counts).astype(jnp.int32)
        slab_starts = slab_ends - slab_counts
        global_slot = jnp.arange(KTOT, dtype=jnp.int32)
        owner_slab = jnp.sum((slab_ends[None, :] <= global_slot[:, None]).astype(jnp.int32), axis=1).astype(jnp.int32)
        position = global_slot - slab_starts[owner_slab]
        local_cell = kinetic_cells[step_index][owner_slab * slab_cells + position]
        global_rows = (owner_slab * slab_cells + local_cell).astype(jnp.int32)
        kin_rows = jnp.moveaxis(flat_rows[:, global_rows, :], 0, 1).reshape(KTOT, NV)
        collided = lax.map(lambda row_block: collide(row_block, map_a, map_b, map_c),
                           kin_rows.astype(jnp.bfloat16).reshape(KTOT // KMEAN, KMEAN, NV)).reshape(KTOT, NV)
        kinetic = kin_rows + COLLIDE * collided.astype(jnp.float32)
        kinetic_grouped = jnp.moveaxis(kinetic.reshape(KTOT, N_VEL, vel_width), 1, 0)
        updated = relaxed.at[:, global_rows, :].set(kinetic_grouped)
        current = updated.reshape(N_VEL, NX, NY, NZ, vel_width)
    return jnp.moveaxis(current, 0, 3).reshape(NX, NY, NZ, NV)
```

```python
import functools
import math

import jax
import jax.numpy as jnp
import numpy as np
from jax import lax
from jax.experimental import pallas as pl
from jax.experimental.pallas import tpu as pltpu
from jax.sharding import PartitionSpec as P

GX = 16
GY = 16
GZ = 8
STEPS = 2
COURANT = 0.1
SPACING = 0.5
COLLIDE = 0.5
LANES = 128
CHUNKS = 8
MESH = pl.DeviceIdType.MESH


def tables():
    k = np.arange(GX * GY * GZ)
    vx = ((k // (GY * GZ)) - 0.5 * (GX - 1)) * SPACING
    vy = (((k // GZ) % GY) - 0.5 * (GY - 1)) * SPACING
    vz = ((k % GZ) - 0.5 * (GZ - 1)) * SPACING
    s = vx * vx + vy * vy + vz * vz
    w = np.exp(-0.5 * s)
    w = w / w.sum()
    m2, m4 = (w * s).sum(), (w * s * s).sum()
    kappa = m4 - m2 * m2
    per_e = w * (s - m2) / kappa
    rows = np.stack([
        w - m2 * per_e,
        w * vx / (w * vx * vx).sum(),
        w * vy / (w * vy * vy).sum(),
        w * vz / (w * vz * vz).sum(),
        per_e,
        per_e,
    ])
    s_hi = np.asarray(np.asarray(s, np.float32).astype(jnp.bfloat16), np.float64)
    cols = np.stack([np.ones_like(vx), vx, vy, vz, s_hi, s - s_hi], axis=1)
    g_hi = np.asarray(np.asarray(rows, np.float32).astype(jnp.bfloat16), np.float64)
    g_lo = rows - g_hi
    basis = np.zeros((24, k.size))
    back = np.zeros((24, k.size))
    for at, part in ((0, g_hi), (8, g_hi), (16, g_lo)):
        basis[at:at + 6] = cols.T
        back[at:at + 6] = part
    return basis.astype(np.float32), back.astype(np.float32)


def limited(a, b):
    return jnp.minimum(jnp.maximum(a, jnp.minimum(b, 0.0)), jnp.maximum(b, 0.0))


def merged(code_row, moved, payload, own_back):
    code = jnp.broadcast_to(code_row, (LANES, LANES)).T
    equilibrium = jnp.dot(payload[:, :LANES], own_back, preferred_element_type=jnp.float32)
    out = []
    for t in range(moved.shape[1] // LANES):
        cols = slice(t * LANES, (t + 1) * LANES)
        old = moved[:, cols]
        fluid = old + code * (equilibrium[:, cols] - old)
        out.append(jnp.where(code < 0.0, old - code * payload[:, cols].astype(jnp.float32), fluid))
    return jnp.concatenate(out, axis=1)


def kernel(dims, counts, kin_cells, relax, basis_rows, back, dist, a_hbm, b_hbm, c_hbm,
           moved_out, ret_out, codes,
           cur, moved, cprev, halo, sendbuf, recv, res, ret, map_a, map_b, map_c, basis, spread,
           load_sem, const_sem, local_sem, out_sem, halo_send, halo_recv, row_send, row_recv, res_send, res_recv):
    nx, ny, nz, width, groups, slabs = dims
    plane = ny * nz
    cells = nx * plane
    chunk = cells // CHUNKS
    rows = chunk // groups
    planes = nx // CHUNKS
    tiles = width // LANES
    me = lax.axis_index("vel")
    slab = lax.axis_index("space")
    first_x = (me * width) // (GY * GZ)
    bit = first_x // (GX // 2)
    sign = 2 * bit - 1
    ahead = lax.rem(slab + sign + slabs, slabs)
    behind = lax.rem(slab - sign + slabs, slabs)

    pieces = [0, CHUNKS - 1] + list(range(1, CHUNKS - 1))
    loads = {}
    for c in pieces:
        loads[c] = pltpu.make_async_copy(
            dist.at[pl.ds(c * chunk, chunk)], cur.at[pl.ds(2 * plane + c * chunk, chunk)], load_sem.at[c])
        loads[c].start()
    consts = []
    for n, (src, dst) in enumerate(((a_hbm, map_a), (b_hbm, map_b), (c_hbm, map_c))):
        consts.append(pltpu.make_async_copy(src, dst, const_sem.at[n]))
        consts[-1].start()

    barrier = pltpu.get_barrier_semaphore()
    for p in range(1, groups):
        pl.semaphore_signal(barrier, inc=1, device_id={"vel": lax.rem(me + p, groups)}, device_id_type=MESH)
    pl.semaphore_signal(barrier, inc=1, device_id={"space": ahead}, device_id_type=MESH)
    pl.semaphore_signal(barrier, inc=1, device_id={"space": behind}, device_id_type=MESH)
    pl.semaphore_wait(barrier, groups + 1)

    @pl.loop(0, basis.shape[0] // LANES)
    def _(n):
        here = pl.ds(pl.multiple_of(n * LANES, LANES), LANES)
        part = basis_rows[:, here]
        whole = jnp.concatenate([part, jnp.zeros((LANES - part.shape[0], LANES), jnp.float32)], axis=0)
        basis[here] = whole.T.astype(jnp.bfloat16)

    groups_of = cells // LANES
    span = 4 * LANES
    for step in range(STEPS):
        count = counts[step, slab]
        flags = jnp.zeros((groups_of, LANES), jnp.float32)
        for n in range(cells // span):
            which = kin_cells[step:step + 1, n * span:(n + 1) * span]
            live = n * span + lax.broadcasted_iota(jnp.int32, (1, span), 1) < count
            quotient = jnp.where(live, lax.div(which, LANES), -1)
            hot_high = lax.broadcasted_iota(jnp.int32, (groups_of, span), 0) == quotient
            hot_low = lax.broadcasted_iota(jnp.int32, (LANES, span), 0) == lax.rem(which, LANES)
            flags += lax.dot_general(
                jnp.where(hot_high, 1.0, 0.0).astype(jnp.bfloat16), jnp.where(hot_low, 1.0, 0.0).astype(jnp.bfloat16),
                (((1,), (1,)), ((), ())), preferred_element_type=jnp.float32)
        codes[step] = jnp.where(flags > 0.5, -COLLIDE, relax[...])

    lane = lax.broadcasted_iota(jnp.int32, (1, LANES), 1)
    vy = (((lane // GZ) % GY).astype(jnp.float32) - 0.5 * (GY - 1)) * SPACING
    vz = ((lane % GZ).astype(jnp.float32) - 0.5 * (GZ - 1)) * SPACING
    block = (nz, LANES)
    pos_y = jnp.broadcast_to(vy > 0.0, block)
    pos_z = jnp.broadcast_to(vz > 0.0, block)
    half_y = jnp.broadcast_to(jnp.where(vy > 0.0, 0.5, -0.5), block)
    half_z = jnp.broadcast_to(jnp.where(vz > 0.0, 0.5, -0.5), block)
    rate_y = jnp.broadcast_to(COURANT * jnp.abs(vy), block)
    rate_z = jnp.broadcast_to(COURANT * jnp.abs(vz), block)

    def pick(positive, negative):
        return bit * positive + (1 - bit) * negative

    def at(index, y):
        return pl.ds(pl.multiple_of(index * plane + y * nz, nz), nz)

    def x_state(index, y, cols):
        mid = cur[at(index, y), cols]
        slope = limited(mid - cur[at(index - sign, y), cols], cur[at(index + sign, y), cols] - mid)
        return mid + 0.5 * slope

    def transport(c):
        start = pick(2 + c * planes, 2 + (c + 1) * planes - 1)

        @pl.loop(0, ny)
        def _(y):
            for t in range(tiles):
                cols = pl.ds(t * LANES, LANES)
                cprev[pl.ds(pl.multiple_of(y * nz, nz), nz), cols] = x_state(start - sign, y, cols)

        @pl.loop(0, planes)
        def _(j):
            index = start + sign * j
            @pl.loop(0, tiles)
            def _(t):
                cols = pl.ds(pl.multiple_of(t * LANES, LANES), LANES)
                vx = (((me * width + t * LANES) // (GY * GZ)).astype(jnp.float32) - 0.5 * (GX - 1)) * SPACING
                rate_x = COURANT * jnp.abs(vx)

                def value(y):
                    return cur[at(index, y % ny), cols]

                def y_state(mid, before, after):
                    return mid + half_y * limited(before, after)

                f = {y: value(y) for y in range(-2, 2)}
                d = {y: f[y + 1] - f[y] for y in (-2, -1, 0)}
                cy = {y: y_state(f[y], d[y - 1], d[y]) for y in (-1, 0)}
                for y in range(ny):
                    f[y + 2] = value(y + 2)
                    d[y + 1] = f[y + 2] - f[y + 1]
                    cy[y + 1] = y_state(f[y + 1], d[y], d[y + 1])
                    mid = f[y]
                    total = rate_y * (cy[y] - jnp.where(pos_y, cy[y - 1], cy[y + 1]))
                    dz = pltpu.roll(mid, nz - 1, 0) - mid
                    cz = mid + half_z * limited(pltpu.roll(dz, 1, 0), dz)
                    total += rate_z * (cz - jnp.where(pos_z, pltpu.roll(cz, 1, 0), pltpu.roll(cz, nz - 1, 0)))
                    cx = x_state(index, y, cols)
                    here = pl.ds(y * nz, nz)
                    total += rate_x * (cx - cprev[here, cols])
                    cprev[here, cols] = cx
                    result = mid - total
                    moved[at(index - 2, y), cols] = result
                    sendbuf[at(index - 2, y), cols] = result.astype(jnp.bfloat16)

    def row_copies(c):
        out = []
        for p in range(1, groups):
            peer = lax.rem(me + p, groups)
            out.append(pltpu.make_async_remote_copy(
                src_ref=sendbuf.at[pl.ds(pl.multiple_of(c * chunk + peer * rows, rows), rows)],
                dst_ref=recv.at[me, pl.ds(c * rows, rows)],
                send_sem=row_send.at[c, p], recv_sem=row_recv.at[c, p],
                device_id={"vel": peer}, device_id_type=MESH))
        return out

    def row_local(c):
        return pltpu.make_async_copy(
            sendbuf.at[pl.ds(pl.multiple_of(c * chunk + me * rows, rows), rows)],
            recv.at[me, pl.ds(c * rows, rows)], local_sem.at[0, c])

    def res_copies(c):
        out = []
        for p in range(1, groups):
            peer = lax.rem(me + p, groups)
            out.append(pltpu.make_async_remote_copy(
                src_ref=res.at[peer, pl.ds(c * rows, rows)],
                dst_ref=ret.at[pl.ds(pl.multiple_of(c * chunk + me * rows, rows), rows)],
                send_sem=res_send.at[c, p], recv_sem=res_recv.at[c, p],
                device_id={"vel": peer}, device_id_type=MESH))
        return out

    def res_local(c):
        return pltpu.make_async_copy(
            res.at[me, pl.ds(c * rows, rows)],
            ret.at[pl.ds(pl.multiple_of(c * chunk + me * rows, rows), rows)], local_sem.at[1, c])

    def collide(step, c):
        here = pl.ds(c * rows, rows)
        first = second = mom = None
        for s in range(groups):
            part = recv[s, here]
            cols = pl.ds(s * width, width)
            terms = [jnp.dot(part, m[cols], preferred_element_type=jnp.float32) for m in (map_a, map_b, basis)]
            first, second, mom = terms if s == 0 else [old + new for old, new in zip((first, second, mom), terms)]
        hidden = (first * second).astype(jnp.bfloat16)
        high = mom.astype(jnp.bfloat16).astype(jnp.float32)
        is_low = (lax.broadcasted_iota(jnp.int32, mom.shape, 1) // 8) == 1
        split = jnp.where(is_low, mom - high, high)
        begin = c * chunk + me * rows
        spread[...] = jnp.broadcast_to(codes[step, pl.ds(begin // LANES, 1)], (LANES, LANES)).T
        kin = spread[pl.ds(pl.multiple_of(lax.rem(begin, LANES), math.gcd(rows, LANES)), rows)] < 0.0
        for s in range(groups):
            cols = pl.ds(s * width, width)
            out = jnp.dot(hidden, map_c[:, cols], preferred_element_type=jnp.float32)
            res[s, here, :LANES] = jnp.where(kin, out[:, :LANES], split).astype(jnp.bfloat16)
            if tiles > 1:
                res[s, here, LANES:] = out[:, LANES:].astype(jnp.bfloat16)

    def update(step, c):
        own_back = back[...]

        @pl.loop(0, chunk // LANES)
        def _(n):
            base = pl.multiple_of(c * chunk + n * LANES, LANES)
            here = pl.ds(base, LANES)
            cur[pl.ds(2 * plane + base, LANES)] = merged(
                codes[step, pl.ds(c * (chunk // LANES) + n, 1)], moved[here], ret[here], own_back)

    def halo_copies(step):
        two, one = 2 * plane, plane
        ahead_src = pick(nx * plane, 2 * plane)
        behind_src = pick(2 * plane, (nx + 1) * plane)
        return [
            pltpu.make_async_remote_copy(
                src_ref=cur.at[pl.ds(pl.multiple_of(ahead_src, plane), two)], dst_ref=halo.at[step, pl.ds(0, two)],
                send_sem=halo_send.at[0], recv_sem=halo_recv.at[step, 0],
                device_id={"space": ahead}, device_id_type=MESH),
            pltpu.make_async_remote_copy(
                src_ref=cur.at[pl.ds(pl.multiple_of(behind_src, plane), one)], dst_ref=halo.at[step, pl.ds(two, one)],
                send_sem=halo_send.at[1], recv_sem=halo_recv.at[step, 1],
                device_id={"space": behind}, device_id_type=MESH),
        ]

    def halo_place(step):
        two, one = 2 * plane, plane
        up_dst = pick(0, (nx + 2) * plane)
        down_dst = pick((nx + 2) * plane, plane)
        return [
            pltpu.make_async_copy(halo.at[step, pl.ds(0, two)], cur.at[pl.ds(pl.multiple_of(up_dst, plane), two)],
                                  local_sem.at[2, 0]),
            pltpu.make_async_copy(halo.at[step, pl.ds(two, one)], cur.at[pl.ds(pl.multiple_of(down_dst, plane), one)],
                                  local_sem.at[2, 1]),
        ]

    outs = []
    sent, back_sent = {}, {}
    waiting = set()

    def finish(step, c):
        for copy in back_sent[c]:
            copy.wait()
        update(step, c)
        waiting.discard(c)

    def send_rows(step, c):
        sent[c] = row_copies(c)
        for copy in sent[c]:
            copy.start()
        own_copy = row_local(c)
        own_copy.start()
        sent[c].append(own_copy)
        if step == STEPS - 1:
            outs.append(pltpu.make_async_copy(
                moved.at[pl.ds(c * chunk, chunk)], moved_out.at[pl.ds(c * chunk, chunk)], out_sem.at[0, c]))
            outs[-1].start()

    def collide_send(step, c):
        for copy in sent[c]:
            copy.wait()
        collide(step, c)
        back_sent[c] = res_copies(c)
        for copy in back_sent[c]:
            copy.start()
        own_copy = res_local(c)
        own_copy.start()
        back_sent[c].append(own_copy)

    edges = [0, CHUNKS - 1]
    order = list(range(1, CHUNKS - 1)) + edges
    later = list(range(2, CHUNKS - 2)) + [1, CHUNKS - 2] + edges
    for step in range(STEPS):
        if step == 0:
            for c in edges:
                loads[c].wait()
            halos = halo_copies(step)
            for copy in halos:
                copy.start()
            loaded = set(edges)
        else:
            halos = None
            order = later
        for n, c in enumerate(order):
            near = [k for k in (c - 1, c, c + 1) if 0 <= k < CHUNKS]
            if step == 0:
                for k in near:
                    if k not in loaded:
                        loads[k].wait()
                        loaded.add(k)
            else:
                if n == CHUNKS - 4:
                    near = sorted(waiting)
                for k in near:
                    if k in waiting:
                        finish(step - 1, k)
                if halos is None and not waiting.intersection(edges):
                    halos = halo_copies(step)
                    for copy in halos:
                        copy.start()
            if n == CHUNKS - 2:
                for copy in halos:
                    copy.wait()
                places = halo_place(step)
                for copy in places:
                    copy.start()
                for copy in places:
                    copy.wait()
            transport(c)
            send_rows(step, c)
            if step == 0 and n == 0:
                for copy in consts:
                    copy.wait()
            if n > 0:
                collide_send(step, order[n - 1])
        collide_send(step, order[-1])
        waiting = set(order)
    for c in order:
        for copy in back_sent[c]:
            copy.wait()
        outs.append(pltpu.make_async_copy(
            ret.at[pl.ds(c * chunk, chunk)], ret_out.at[pl.ds(c * chunk, chunk)], out_sem.at[1, c]))
        outs[-1].start()
    for copy in outs:
        copy.wait()


def final_kernel(codes, moved_ref, ret_ref, back_ref, out_ref):
    at = pl.program_id(0) * (out_ref.shape[0] // LANES)
    for n in range(out_ref.shape[0] // LANES):
        here = pl.ds(n * LANES, LANES)
        out_ref[here] = merged(codes[STEPS - 1, pl.ds(at + n, 1)], moved_ref[here], ret_ref[here], back_ref[...])


def body(dist, relax_rate, kinetic_cells, kinetic_count, map_a, map_b, map_c):
    nx, ny, nz, width = dist.shape
    groups = lax.axis_size("vel")
    slabs = lax.axis_size("space")
    cells = nx * ny * nz
    chunk = cells // CHUNKS
    rows = chunk // groups
    plane = ny * nz
    basis, back = tables()
    back = lax.dynamic_slice_in_dim(jnp.asarray(back), lax.axis_index("vel") * width, width, 1)
    back = jnp.pad(back, ((0, LANES - back.shape[0]), (0, 0))).astype(jnp.bfloat16)

    any_space = pl.BlockSpec(memory_space=pl.ANY)
    f32, bf16 = jnp.float32, jnp.bfloat16
    dims = (nx, ny, nz, width, groups, slabs)
    vmem = pl.BlockSpec(memory_space=pltpu.VMEM)
    moved, ret, codes = pl.pallas_call(
        functools.partial(kernel, dims),
        out_shape=(jax.ShapeDtypeStruct((cells, width), f32), jax.ShapeDtypeStruct((cells, width), bf16),
                   jax.ShapeDtypeStruct((STEPS, cells // LANES, LANES), f32)),
        in_specs=[pl.BlockSpec(memory_space=pltpu.SMEM)] + [vmem] * 4 + [any_space] * 4,
        out_specs=(any_space, any_space, vmem),
        scratch_shapes=[
            pltpu.VMEM(((nx + 4) * plane, width), f32),
            pltpu.VMEM((cells, width), f32),
            pltpu.VMEM((plane, width), f32),
            pltpu.VMEM((STEPS, 3 * plane, width), f32),
            pltpu.VMEM((cells, width), bf16),
            pltpu.VMEM((groups, CHUNKS * rows, width), bf16),
            pltpu.VMEM((groups, CHUNKS * rows, width), bf16),
            pltpu.VMEM((cells, width), bf16),
            pltpu.VMEM(map_a.shape, bf16),
            pltpu.VMEM(map_b.shape, bf16),
            pltpu.VMEM(map_c.shape, bf16),
            pltpu.VMEM((map_a.shape[0], LANES), bf16),
            pltpu.VMEM((LANES, LANES), f32),
            pltpu.SemaphoreType.DMA((CHUNKS,)),
            pltpu.SemaphoreType.DMA((3,)),
            pltpu.SemaphoreType.DMA((3, CHUNKS)),
            pltpu.SemaphoreType.DMA((2, CHUNKS)),
            pltpu.SemaphoreType.DMA((2,)),
            pltpu.SemaphoreType.DMA((STEPS, 2)),
            pltpu.SemaphoreType.DMA((CHUNKS, groups)),
            pltpu.SemaphoreType.DMA((CHUNKS, groups)),
            pltpu.SemaphoreType.DMA((CHUNKS, groups)),
            pltpu.SemaphoreType.DMA((CHUNKS, groups)),
        ],
        compiler_params=pltpu.CompilerParams(
            collective_id=0, has_side_effects=True, vmem_limit_bytes=67043328),
    )(kinetic_count, kinetic_cells, relax_rate.reshape(cells // LANES, LANES), jnp.asarray(basis), back,
      dist.reshape(cells, width), map_a, map_b, map_c)

    size = cells // 8
    out = pl.pallas_call(
        final_kernel,
        grid=(8,),
        out_shape=jax.ShapeDtypeStruct((cells, width), f32),
        in_specs=[
            pl.BlockSpec((STEPS, cells // LANES, LANES), lambda i: (0, 0, 0)),
            pl.BlockSpec((size, width), lambda i: (i, 0)),
            pl.BlockSpec((size, width), lambda i: (i, 0)),
            pl.BlockSpec((LANES, width), lambda i: (0, 0)),
        ],
        out_specs=pl.BlockSpec((size, width), lambda i: (i, 0)),
    )(codes, moved, ret, back)
    return out.reshape(dist.shape)


def solution(mesh):
    return jax.shard_map(
        body,
        mesh=mesh,
        in_specs=(
            P("space", None, None, "vel"),
            P("space", None, None),
            P(None, "space"),
            P(),
            P(),
            P(),
            P(),
        ),
        out_specs=P("space", None, None, "vel"),
        check_vma=False,
    )
```

```python
import functools
import math

import jax
import jax.numpy as jnp
import numpy as np
from jax import lax
from jax.experimental import pallas as pl
from jax.experimental.pallas import tpu as pltpu
from jax.sharding import PartitionSpec as P

GX = 16
GY = 16
GZ = 8
STEPS = 2
COURANT = 0.1
SPACING = 0.5
COLLIDE = 0.5
LANES = 128
CHUNKS = 4
LAG = 1
MESH = pl.DeviceIdType.MESH


def tables():
    k = np.arange(GX * GY * GZ)
    vx = ((k // (GY * GZ)) - 0.5 * (GX - 1)) * SPACING
    vy = (((k // GZ) % GY) - 0.5 * (GY - 1)) * SPACING
    vz = ((k % GZ) - 0.5 * (GZ - 1)) * SPACING
    s = vx * vx + vy * vy + vz * vz
    w = np.exp(-0.5 * s)
    w = w / w.sum()
    m2, m4 = (w * s).sum(), (w * s * s).sum()
    kappa = m4 - m2 * m2
    per_e = w * (s - m2) / kappa
    rows = np.stack([
        w - m2 * per_e,
        w * vx / (w * vx * vx).sum(),
        w * vy / (w * vy * vy).sum(),
        w * vz / (w * vz * vz).sum(),
        per_e,
        per_e,
    ])
    s_hi = np.asarray(np.asarray(s, np.float32).astype(jnp.bfloat16), np.float64)
    cols = np.stack([np.ones_like(vx), vx, vy, vz, s_hi, s - s_hi], axis=1)
    g_hi = np.asarray(np.asarray(rows, np.float32).astype(jnp.bfloat16), np.float64)
    g_lo = rows - g_hi
    basis = np.zeros((24, k.size))
    back = np.zeros((24, k.size))
    for at, part in ((0, g_hi), (8, g_hi), (16, g_lo)):
        basis[at:at + 6] = cols.T
        back[at:at + 6] = part
    return basis.astype(np.float32), back.astype(np.float32)


def limited(a, b):
    return jnp.minimum(jnp.maximum(a, jnp.minimum(b, 0.0)), jnp.maximum(b, 0.0))


def merged(code_row, moved, payload, own_back):
    code = jnp.broadcast_to(code_row, (LANES, LANES)).T
    equilibrium = jnp.dot(payload[:, :LANES], own_back, preferred_element_type=jnp.float32)
    out = []
    for t in range(moved.shape[1] // LANES):
        cols = slice(t * LANES, (t + 1) * LANES)
        old = moved[:, cols]
        fluid = old + code * (equilibrium[:, cols] - old)
        out.append(jnp.where(code < 0.0, old - code * payload[:, cols].astype(jnp.float32), fluid))
    return jnp.concatenate(out, axis=1)


def kernel(dims, counts, kin_cells, relax, basis_rows, back, dist, a_hbm, b_hbm, c_hbm,
           moved_out, ret_out, codes,
           cur, moved, cprev, halo, sendbuf, recv, res, ret, map_a, map_b, map_c, basis, spread,
           load_sem, const_sem, local_sem, out_sem, halo_send, halo_recv, row_send, row_recv, res_send, res_recv):
    nx, ny, nz, width, groups, slabs = dims
    plane = ny * nz
    cells = nx * plane
    chunk = cells // CHUNKS
    rows = chunk // groups
    planes = nx // CHUNKS
    tiles = width // LANES
    me = lax.axis_index("vel")
    slab = lax.axis_index("space")
    first_x = (me * width) // (GY * GZ)
    bit = first_x // (GX // 2)
    sign = 2 * bit - 1
    ahead = lax.rem(slab + sign + slabs, slabs)
    behind = lax.rem(slab - sign + slabs, slabs)

    pieces = [0, CHUNKS - 1] + list(range(1, CHUNKS - 1))
    loads = {}
    for c in pieces:
        loads[c] = pltpu.make_async_copy(
            dist.at[pl.ds(c * chunk, chunk)], cur.at[pl.ds(2 * plane + c * chunk, chunk)], load_sem.at[c])
        loads[c].start()
    consts = []
    for n, (src, dst) in enumerate(((a_hbm, map_a), (b_hbm, map_b), (c_hbm, map_c))):
        consts.append(pltpu.make_async_copy(src, dst, const_sem.at[n]))
        consts[-1].start()

    barrier = pltpu.get_barrier_semaphore()
    for p in range(1, groups):
        pl.semaphore_signal(barrier, inc=1, device_id={"vel": lax.rem(me + p, groups)}, device_id_type=MESH)
    pl.semaphore_signal(barrier, inc=1, device_id={"space": ahead}, device_id_type=MESH)
    pl.semaphore_signal(barrier, inc=1, device_id={"space": behind}, device_id_type=MESH)
    pl.semaphore_wait(barrier, groups + 1)

    lane = lax.broadcasted_iota(jnp.int32, (1, LANES), 1)
    vy = (((lane // GZ) % GY).astype(jnp.float32) - 0.5 * (GY - 1)) * SPACING
    vz = ((lane % GZ).astype(jnp.float32) - 0.5 * (GZ - 1)) * SPACING
    block = (nz, LANES)
    pos_y = jnp.broadcast_to(vy > 0.0, block)
    pos_z = jnp.broadcast_to(vz > 0.0, block)
    half_y = jnp.broadcast_to(jnp.where(vy > 0.0, 0.5, -0.5), block)
    half_z = jnp.broadcast_to(jnp.where(vz > 0.0, 0.5, -0.5), block)
    rate_y = jnp.broadcast_to(COURANT * jnp.abs(vy), block)
    rate_z = jnp.broadcast_to(COURANT * jnp.abs(vz), block)

    def pick(positive, negative):
        return bit * positive + (1 - bit) * negative

    def at(index, y):
        return pl.ds(pl.multiple_of(index * plane + y * nz, nz), nz)

    def x_state(index, y, cols):
        mid = cur[at(index, y), cols]
        slope = limited(mid - cur[at(index - sign, y), cols], cur[at(index + sign, y), cols] - mid)
        return mid + 0.5 * slope

    def transport(c):
        start = pick(2 + c * planes, 2 + (c + 1) * planes - 1)

        @pl.loop(0, ny)
        def _(y):
            for t in range(tiles):
                cols = pl.ds(t * LANES, LANES)
                cprev[pl.ds(pl.multiple_of(y * nz, nz), nz), cols] = x_state(start - sign, y, cols)

        @pl.loop(0, planes)
        def _(j):
            index = start + sign * j
            @pl.loop(0, tiles)
            def _(t):
                cols = pl.ds(pl.multiple_of(t * LANES, LANES), LANES)
                vx = (((me * width + t * LANES) // (GY * GZ)).astype(jnp.float32) - 0.5 * (GX - 1)) * SPACING
                rate_x = COURANT * jnp.abs(vx)

                def value(y):
                    return cur[at(index, y % ny), cols]

                def y_state(mid, before, after):
                    return mid + half_y * limited(before, after)

                f = {y: value(y) for y in range(-2, 2)}
                d = {y: f[y + 1] - f[y] for y in (-2, -1, 0)}
                cy = {y: y_state(f[y], d[y - 1], d[y]) for y in (-1, 0)}
                for y in range(ny):
                    f[y + 2] = value(y + 2)
                    d[y + 1] = f[y + 2] - f[y + 1]
                    cy[y + 1] = y_state(f[y + 1], d[y], d[y + 1])
                    mid = f[y]
                    total = rate_y * (cy[y] - jnp.where(pos_y, cy[y - 1], cy[y + 1]))
                    dz = pltpu.roll(mid, nz - 1, 0) - mid
                    cz = mid + half_z * limited(pltpu.roll(dz, 1, 0), dz)
                    total += rate_z * (cz - jnp.where(pos_z, pltpu.roll(cz, 1, 0), pltpu.roll(cz, nz - 1, 0)))
                    cx = x_state(index, y, cols)
                    here = pl.ds(y * nz, nz)
                    total += rate_x * (cx - cprev[here, cols])
                    cprev[here, cols] = cx
                    result = mid - total
                    moved[at(index - 2, y), cols] = result
                    sendbuf[at(index - 2, y), cols] = result.astype(jnp.bfloat16)

    def prepare():
        @pl.loop(0, basis.shape[0] // LANES)
        def _(n):
            here = pl.ds(pl.multiple_of(n * LANES, LANES), LANES)
            part = basis_rows[:, here]
            whole = jnp.concatenate([part, jnp.zeros((LANES - part.shape[0], LANES), jnp.float32)], axis=0)
            basis[here] = whole.T.astype(jnp.bfloat16)

        groups_of = cells // LANES
        span = 4 * LANES
        for step in range(STEPS):
            count = counts[step, slab]
            flags = jnp.zeros((groups_of, LANES), jnp.float32)
            for n in range(cells // span):
                which = kin_cells[step:step + 1, n * span:(n + 1) * span]
                live = n * span + lax.broadcasted_iota(jnp.int32, (1, span), 1) < count
                quotient = jnp.where(live, lax.div(which, LANES), -1)
                hot_high = lax.broadcasted_iota(jnp.int32, (groups_of, span), 0) == quotient
                hot_low = lax.broadcasted_iota(jnp.int32, (LANES, span), 0) == lax.rem(which, LANES)
                flags += lax.dot_general(
                    jnp.where(hot_high, 1.0, 0.0).astype(jnp.bfloat16), jnp.where(hot_low, 1.0, 0.0).astype(jnp.bfloat16),
                    (((1,), (1,)), ((), ())), preferred_element_type=jnp.float32)
            codes[step] = jnp.where(flags > 0.5, -COLLIDE, relax[...])

    def row_copies(c):
        out = []
        for p in range(1, groups):
            peer = lax.rem(me + p, groups)
            out.append(pltpu.make_async_remote_copy(
                src_ref=sendbuf.at[pl.ds(pl.multiple_of(c * chunk + peer * rows, rows), rows)],
                dst_ref=recv.at[me, pl.ds(c * rows, rows)],
                send_sem=row_send.at[c, p], recv_sem=row_recv.at[c, p],
                device_id={"vel": peer}, device_id_type=MESH))
        return out

    def row_local(c):
        return pltpu.make_async_copy(
            sendbuf.at[pl.ds(pl.multiple_of(c * chunk + me * rows, rows), rows)],
            recv.at[me, pl.ds(c * rows, rows)], local_sem.at[0, c])

    def res_copies(c):
        out = []
        for p in range(1, groups):
            peer = lax.rem(me + p, groups)
            out.append(pltpu.make_async_remote_copy(
                src_ref=res.at[peer, pl.ds(c * rows, rows)],
                dst_ref=ret.at[pl.ds(pl.multiple_of(c * chunk + me * rows, rows), rows)],
                send_sem=res_send.at[c, p], recv_sem=res_recv.at[c, p],
                device_id={"vel": peer}, device_id_type=MESH))
        return out

    def res_local(c):
        return pltpu.make_async_copy(
            res.at[me, pl.ds(c * rows, rows)],
            ret.at[pl.ds(pl.multiple_of(c * chunk + me * rows, rows), rows)], local_sem.at[1, c])

    def collide(step, c):
        here = pl.ds(c * rows, rows)
        first = second = mom = None
        for s in range(groups):
            part = recv[s, here]
            cols = pl.ds(s * width, width)
            terms = [jnp.dot(part, m[cols], preferred_element_type=jnp.float32) for m in (map_a, map_b, basis)]
            first, second, mom = terms if s == 0 else [old + new for old, new in zip((first, second, mom), terms)]
        hidden = (first * second).astype(jnp.bfloat16)
        high = mom.astype(jnp.bfloat16).astype(jnp.float32)
        is_low = (lax.broadcasted_iota(jnp.int32, mom.shape, 1) // 8) == 1
        split = jnp.where(is_low, mom - high, high)
        begin = c * chunk + me * rows
        spread[...] = jnp.broadcast_to(codes[step, pl.ds(begin // LANES, 1)], (LANES, LANES)).T
        kin = spread[pl.ds(pl.multiple_of(lax.rem(begin, LANES), math.gcd(rows, LANES)), rows)] < 0.0
        for s in range(groups):
            cols = pl.ds(s * width, width)
            out = jnp.dot(hidden, map_c[:, cols], preferred_element_type=jnp.float32)
            res[s, here, :LANES] = jnp.where(kin, out[:, :LANES], split).astype(jnp.bfloat16)
            if tiles > 1:
                res[s, here, LANES:] = out[:, LANES:].astype(jnp.bfloat16)

    def update(step, c):
        own_back = back[...]

        @pl.loop(0, chunk // LANES)
        def _(n):
            base = pl.multiple_of(c * chunk + n * LANES, LANES)
            here = pl.ds(base, LANES)
            cur[pl.ds(2 * plane + base, LANES)] = merged(
                codes[step, pl.ds(c * (chunk // LANES) + n, 1)], moved[here], ret[here], own_back)

    def halo_copies(step):
        two, one = 2 * plane, plane
        ahead_src = pick(nx * plane, 2 * plane)
        behind_src = pick(2 * plane, (nx + 1) * plane)
        return [
            pltpu.make_async_remote_copy(
                src_ref=cur.at[pl.ds(pl.multiple_of(ahead_src, plane), two)], dst_ref=halo.at[step, pl.ds(0, two)],
                send_sem=halo_send.at[0], recv_sem=halo_recv.at[step, 0],
                device_id={"space": ahead}, device_id_type=MESH),
            pltpu.make_async_remote_copy(
                src_ref=cur.at[pl.ds(pl.multiple_of(behind_src, plane), one)], dst_ref=halo.at[step, pl.ds(two, one)],
                send_sem=halo_send.at[1], recv_sem=halo_recv.at[step, 1],
                device_id={"space": behind}, device_id_type=MESH),
        ]

    def halo_place(step):
        two, one = 2 * plane, plane
        up_dst = pick(0, (nx + 2) * plane)
        down_dst = pick((nx + 2) * plane, plane)
        return [
            pltpu.make_async_copy(halo.at[step, pl.ds(0, two)], cur.at[pl.ds(pl.multiple_of(up_dst, plane), two)],
                                  local_sem.at[2, 0]),
            pltpu.make_async_copy(halo.at[step, pl.ds(two, one)], cur.at[pl.ds(pl.multiple_of(down_dst, plane), one)],
                                  local_sem.at[2, 1]),
        ]

    outs = []
    sent, back_sent = {}, {}
    waiting = set()

    def finish(step, c):
        for copy in back_sent[c]:
            copy.wait()
        update(step, c)
        waiting.discard(c)

    def send_rows(step, c):
        sent[c] = row_copies(c)
        for copy in sent[c]:
            copy.start()
        own_copy = row_local(c)
        own_copy.start()
        sent[c].append(own_copy)
        if step == STEPS - 1:
            outs.append(pltpu.make_async_copy(
                moved.at[pl.ds(c * chunk, chunk)], moved_out.at[pl.ds(c * chunk, chunk)], out_sem.at[0, c]))
            outs[-1].start()

    def collide_send(step, c):
        for copy in sent[c]:
            copy.wait()
        collide(step, c)
        back_sent[c] = res_copies(c)
        for copy in back_sent[c]:
            copy.start()
        own_copy = res_local(c)
        own_copy.start()
        back_sent[c].append(own_copy)

    edges = [0, CHUNKS - 1]
    order = list(range(1, CHUNKS - 1)) + edges
    later = list(range(2, CHUNKS - 2)) + [1, CHUNKS - 2] + edges
    for step in range(STEPS):
        if step == 0:
            for c in edges:
                loads[c].wait()
            halos = halo_copies(step)
            for copy in halos:
                copy.start()
            loaded = set(edges)
        else:
            halos = None
            order = later
        queue = []
        for n, c in enumerate(order):
            near = [k for k in (c - 1, c, c + 1) if 0 <= k < CHUNKS]
            if step == 0:
                for k in near:
                    if k not in loaded:
                        loads[k].wait()
                        loaded.add(k)
            else:
                if n == max(CHUNKS - 4, 1):
                    near = sorted(waiting)
                for k in near:
                    if k in waiting:
                        finish(step - 1, k)
                if halos is None and not waiting.intersection(edges):
                    halos = halo_copies(step)
                    for copy in halos:
                        copy.start()
            if n == CHUNKS - 2:
                for copy in halos:
                    copy.wait()
                places = halo_place(step)
                for copy in places:
                    copy.start()
                for copy in places:
                    copy.wait()
            transport(c)
            send_rows(step, c)
            if step == 0 and n == 0:
                prepare()
                for copy in consts:
                    copy.wait()
            queue.append(c)
            if len(queue) > LAG:
                collide_send(step, queue.pop(0))
        while queue:
            collide_send(step, queue.pop(0))
        waiting = set(order)
    for c in order:
        for copy in back_sent[c]:
            copy.wait()
        outs.append(pltpu.make_async_copy(
            ret.at[pl.ds(c * chunk, chunk)], ret_out.at[pl.ds(c * chunk, chunk)], out_sem.at[1, c]))
        outs[-1].start()
    for copy in outs:
        copy.wait()


def final_kernel(codes, moved_ref, ret_ref, back_ref, out_ref):
    at = pl.program_id(0) * (out_ref.shape[0] // LANES)
    for n in range(out_ref.shape[0] // LANES):
        here = pl.ds(n * LANES, LANES)
        out_ref[here] = merged(codes[STEPS - 1, pl.ds(at + n, 1)], moved_ref[here], ret_ref[here], back_ref[...])


def body(dist, relax_rate, kinetic_cells, kinetic_count, map_a, map_b, map_c):
    nx, ny, nz, width = dist.shape
    groups = lax.axis_size("vel")
    slabs = lax.axis_size("space")
    cells = nx * ny * nz
    chunk = cells // CHUNKS
    rows = chunk // groups
    plane = ny * nz
    basis, back = tables()
    back = lax.dynamic_slice_in_dim(jnp.asarray(back), lax.axis_index("vel") * width, width, 1)
    back = jnp.pad(back, ((0, LANES - back.shape[0]), (0, 0))).astype(jnp.bfloat16)

    any_space = pl.BlockSpec(memory_space=pl.ANY)
    f32, bf16 = jnp.float32, jnp.bfloat16
    dims = (nx, ny, nz, width, groups, slabs)
    vmem = pl.BlockSpec(memory_space=pltpu.VMEM)
    moved, ret, codes = pl.pallas_call(
        functools.partial(kernel, dims),
        out_shape=(jax.ShapeDtypeStruct((cells, width), f32), jax.ShapeDtypeStruct((cells, width), bf16),
                   jax.ShapeDtypeStruct((STEPS, cells // LANES, LANES), f32)),
        in_specs=[pl.BlockSpec(memory_space=pltpu.SMEM)] + [vmem] * 4 + [any_space] * 4,
        out_specs=(any_space, any_space, vmem),
        scratch_shapes=[
            pltpu.VMEM(((nx + 4) * plane, width), f32),
            pltpu.VMEM((cells, width), f32),
            pltpu.VMEM((plane, width), f32),
            pltpu.VMEM((STEPS, 3 * plane, width), f32),
            pltpu.VMEM((cells, width), bf16),
            pltpu.VMEM((groups, CHUNKS * rows, width), bf16),
            pltpu.VMEM((groups, CHUNKS * rows, width), bf16),
            pltpu.VMEM((cells, width), bf16),
            pltpu.VMEM(map_a.shape, bf16),
            pltpu.VMEM(map_b.shape, bf16),
            pltpu.VMEM(map_c.shape, bf16),
            pltpu.VMEM((map_a.shape[0], LANES), bf16),
            pltpu.VMEM((LANES, LANES), f32),
            pltpu.SemaphoreType.DMA((CHUNKS,)),
            pltpu.SemaphoreType.DMA((3,)),
            pltpu.SemaphoreType.DMA((3, CHUNKS)),
            pltpu.SemaphoreType.DMA((2, CHUNKS)),
            pltpu.SemaphoreType.DMA((2,)),
            pltpu.SemaphoreType.DMA((STEPS, 2)),
            pltpu.SemaphoreType.DMA((CHUNKS, groups)),
            pltpu.SemaphoreType.DMA((CHUNKS, groups)),
            pltpu.SemaphoreType.DMA((CHUNKS, groups)),
            pltpu.SemaphoreType.DMA((CHUNKS, groups)),
        ],
        compiler_params=pltpu.CompilerParams(
            collective_id=0, has_side_effects=True, vmem_limit_bytes=67043328),
    )(kinetic_count, kinetic_cells, relax_rate.reshape(cells // LANES, LANES), jnp.asarray(basis), back,
      dist.reshape(cells, width), map_a, map_b, map_c)

    size = cells // 8
    out = pl.pallas_call(
        final_kernel,
        grid=(8,),
        out_shape=jax.ShapeDtypeStruct((cells, width), f32),
        in_specs=[
            pl.BlockSpec((STEPS, cells // LANES, LANES), lambda i: (0, 0, 0)),
            pl.BlockSpec((size, width), lambda i: (i, 0)),
            pl.BlockSpec((size, width), lambda i: (i, 0)),
            pl.BlockSpec((LANES, width), lambda i: (0, 0)),
        ],
        out_specs=pl.BlockSpec((size, width), lambda i: (i, 0)),
    )(codes, moved, ret, back)
    return out.reshape(dist.shape)


def solution(mesh):
    return jax.shard_map(
        body,
        mesh=mesh,
        in_specs=(
            P("space", None, None, "vel"),
            P("space", None, None),
            P(None, "space"),
            P(),
            P(),
            P(),
            P(),
        ),
        out_specs=P("space", None, None, "vel"),
        check_vma=False,
    )
```
